256 devices in a mesh: task: 8 (over x, core), fsdp: 32 (over z, y).
Axes of the slice: x: 4, y: 4, z: 8, core: 2. Of those that a mesh axis runs over, the one named last changes fastest.
Arguments:
- grads_first: bfloat16 [16, 4096, 4096], P('task', 'fsdp'), may hold values from -120 to 120
- weights_first: float32 [4096, 4096], P('fsdp', 'task'), may hold values from -6 to 6
- moment_first: float32 [4096, 4096], P('fsdp', 'task'), may hold values from -3 to 3
- variance_first: float32 [4096, 4096], P('fsdp', 'task'), may hold values from 0.0025 to 1
- grads_second: bfloat16 [16, 4096, 4096], P('task', 'fsdp'), may hold values from -120 to 120
- weights_second: float32 [4096, 4096], P('fsdp', 'task'), may hold values from -6 to 6
- moment_second: float32 [4096, 4096], P('fsdp', 'task'), may hold values from -3 to 3
- variance_second: float32 [4096, 4096], P('fsdp', 'task'), may hold values from 0.0025 to 1
Outputs:
- combined_first: float32 [4096, 4096], P('fsdp', 'task')
- new_weights_first: float32 [4096, 4096], P('fsdp', 'task')
- new_moment_first: float32 [4096, 4096], P('fsdp', 'task')
- new_variance_first: float32 [4096, 4096], P('fsdp', 'task')
- combined_second: float32 [4096, 4096], P('fsdp', 'task')
- new_weights_second: float32 [4096, 4096], P('fsdp', 'task')
- new_moment_second: float32 [4096, 4096], P('fsdp', 'task')
- new_variance_second: float32 [4096, 4096], P('fsdp', 'task')
The draws below stay inside these ranges and needn't reach their ends.
All inputs are finite; a program needn't handle non-finite values.
Results may differ from the reference program's by a relative error of at most 0.0006.
Values may be sent and summed in bfloat16 or wider, within the bound.
A program may use at most 128 MiB of HBM per device.

```python
import math
import jax
import jax.numpy as jnp
from jax import lax

D = 4096
TASKS = 16
ITERS = 20
ROWS = 4096


def grad_field(key, draw_salt):
    folded = jax.random.fold_in(key, draw_salt)
    subkeys = jax.random.split(folded, 10)
    task_scale = jnp.exp(jax.random.uniform(subkeys[0], (TASKS,), jnp.float32, math.log(0.7), math.log(1.4)))
    order = jax.random.permutation(subkeys[7], TASKS)
    task_sign = jnp.where(order < TASKS // 2, 1.0, -1.0).astype(jnp.float32)
    position = jnp.arange(ROWS, dtype=jnp.float32) / ROWS
    row_trend = jnp.exp(math.log(3.0) * (position - 0.5))
    column_position = jnp.arange(D, dtype=jnp.float32) / D
    region = jnp.arange(ROWS, dtype=jnp.int32) * 8 // ROWS
    region_scale = jnp.exp(jax.random.uniform(subkeys[1], (TASKS, 8), jnp.float32, math.log(0.5), math.log(2.0)))
    task_region = region_scale[:, region]
    task_row = jnp.exp(jax.random.uniform(subkeys[2], (TASKS, ROWS), jnp.float32, math.log(0.3), math.log(3.0)))
    task_column = jnp.exp(jax.random.uniform(subkeys[3], (TASKS, D), jnp.float32, math.log(0.3), math.log(3.0)))
    shared_row = jnp.exp(jax.random.uniform(subkeys[8], (ROWS,), jnp.float32, math.log(0.3), math.log(3.0)))
    shared_column = jnp.exp(jax.random.uniform(subkeys[9], (D,), jnp.float32, math.log(0.3), math.log(3.0)))
    common_noise = jnp.clip(jax.random.normal(subkeys[5], (ROWS, D), jnp.float32), -3.5, 3.5)
    independent = 0.3 * jnp.clip(jax.random.normal(subkeys[4], (TASKS, ROWS, D), jnp.float32), -3.5, 3.5)
    alignment = task_sign
    column_trend = jnp.exp(math.log(3.0) * (column_position - 0.5))
    common_part = common_noise * shared_row[:, None] * (shared_column * column_trend)[None, :]
    task_factor = task_region * task_row
    own_part = independent * task_factor[:, :, None] * task_column[:, None, :]
    fluctuation = alignment[:, None, None] * common_part[None, :, :] + own_part
    return 0.25 * task_scale[:, None, None] * row_trend[None, :, None] * fluctuation


def draw_grads_first(key, part):
    return grad_field(key, 11).astype(jnp.bfloat16)


def draw_grads_second(key, part):
    return grad_field(key, 23).astype(jnp.bfloat16)


def block_scale(own_key, extent, cuts, low, largest):
    gain = 1.0
    for axis_at, parts in cuts:
        draws = jax.random.uniform(jax.random.fold_in(jax.random.fold_in(own_key, 6), axis_at), (parts,), jnp.float32, low / len(cuts), largest / len(cuts))
        gain = gain * jnp.repeat(jnp.exp(draws), extent[axis_at] // parts).reshape((-1,) + (1,) * (len(extent) - 1 - axis_at))
    return gain


def bell_draw(rng, extent, scale, most, cuts=(), held_as=jnp.bfloat16):
    array = jax.random.normal(rng, extent, jnp.float32) * scale
    if len(cuts) > 0:
        array = block_scale(rng, extent, cuts, -0.22, 0.18) * array
    return jnp.clip(array, min=-most, max=most).astype(held_as)


def setup_inputs(seed: int = 0) -> dict:
    key_of = jax.random.split(jax.random.key(seed), 9)
    grads_first = draw_grads_first(jax.random.fold_in(key_of[8], 71), 0)
    weights_first = bell_draw(key_of[1], (ROWS, D), 1.0, 6.0, ((0, 32), (1, 8)), jnp.float32)
    moment_first = bell_draw(key_of[2], (ROWS, D), 0.5, 3.0, ((0, 32), (1, 8)), jnp.float32)
    variance_first = jnp.clip(jnp.exp(math.log(1.0) - 5.9914646 * jax.random.uniform(key_of[3], (ROWS, D), jnp.float32) ** block_scale(key_of[3], (ROWS, D), ((0, 32), (1, 8)), -0.2, 0.2)), 0.0025, 1.0)
    grads_second = draw_grads_second(jax.random.fold_in(key_of[8], 71), 0)
    weights_second = bell_draw(key_of[5], (ROWS, D), 1.0, 6.0, ((0, 32), (1, 8)), jnp.float32)
    moment_second = bell_draw(key_of[6], (ROWS, D), 0.5, 3.0, ((0, 32), (1, 8)), jnp.float32)
    variance_second = jnp.clip(jnp.exp(math.log(1.0) - 5.9914646 * jax.random.uniform(key_of[7], (ROWS, D), jnp.float32) ** block_scale(key_of[7], (ROWS, D), ((0, 32), (1, 8)), -0.2, 0.2)), 0.0025, 1.0)
    return dict(grads_first=grads_first, weights_first=weights_first, moment_first=moment_first, variance_first=variance_first, grads_second=grads_second, weights_second=weights_second, moment_second=moment_second, variance_second=variance_second)


temper = 0.05
beta_one = 0.9
beta_two = 0.999
learn_rate = 0.001
adam_step = 1000.0
epsilon = 1e-08

def gram_matrix(gradients):
    total_rows = gradients.shape[1]
    block_rows = math.gcd(total_rows, 256)

    def accumulate(index, accumulated):
        offset = (index * block_rows).astype(jnp.int32)
        segment = lax.dynamic_slice_in_dim(gradients, offset, block_rows, 1).astype(jnp.float32)
        return accumulated + jnp.einsum('tre,sre->ts', segment, segment, precision=lax.Precision.HIGHEST)
    return lax.fori_loop(0, total_rows // block_rows, accumulate, jnp.zeros((TASKS, TASKS), jnp.float32))

def frank_wolfe(gram):
    scaled = gram / jnp.max(jnp.diagonal(gram))

    def advance(iteration, mixture):
        slope = 2.0 * jnp.dot(scaled, mixture, precision=lax.Precision.HIGHEST)
        expweights = jnp.exp(-slope / temper)
        vertex = expweights / jnp.sum(expweights)
        stepsize = 2.0 / (jnp.asarray(iteration).astype(jnp.float32) + 2.0)
        return mixture + stepsize * (vertex - mixture)
    start_mix = jnp.full((TASKS,), 1.0 / TASKS, jnp.float32)
    return lax.fori_loop(0, ITERS, advance, start_mix)

def adam_update(weights, moment, variance, combined):
    new_moment = beta_one * moment + (1.0 - beta_one) * combined
    new_variance = beta_two * variance + (1.0 - beta_two) * combined * combined
    corrected = new_moment / (1.0 - beta_one ** adam_step)
    scaled_var = new_variance / (1.0 - beta_two ** adam_step)
    new_weights = weights - learn_rate * corrected / (jnp.sqrt(scaled_var) + epsilon)
    return (new_weights, new_moment, new_variance)

def one_group(gradients, weights, moment, variance):
    mixture = frank_wolfe(gram_matrix(gradients))
    combined = jnp.zeros(weights.shape, jnp.float32)
    for task_index in range(TASKS):
        combined = combined + mixture[task_index] * gradients[task_index].astype(jnp.float32)
    new_weights, new_moment, new_variance = adam_update(weights, moment, variance, combined)
    return (combined, new_weights, new_moment, new_variance)

def reference(grads_first, weights_first, moment_first, variance_first, grads_second, weights_second, moment_second, variance_second):
    first_c, first_w, first_m, first_v = one_group(grads_first, weights_first, moment_first, variance_first)
    second_c, second_w, second_m, second_v = one_group(grads_second, weights_second, moment_second, variance_second)
    return (first_c, first_w, first_m, first_v, second_c, second_w, second_m, second_v)
```

```python
import functools

import jax
import jax.numpy as jnp
from jax import lax
from jax.experimental import pallas as pl
from jax.experimental.pallas import tpu as pltpu
from jax.sharding import PartitionSpec as P

ITERS = 20

temper = 0.05
beta_one = 0.9
beta_two = 0.999
learn_rate = 0.001
adam_step = 1000.0
epsilon = 1e-08

MESH = pl.DeviceIdType.MESH
TASKS = 16
CORES = 2
CHIPS_X = 4
CHIPS_Y = 4
CHIPS_Z = 8
LANES = 128
ROW_BLOCK = 16
PIECES = ((0, 0, 128), (1, 0, 64), (1, 64, 64))


def gram_block(received, first_row, rows):
    sides = [
        received[:, row : row + ROW_BLOCK, :].reshape(TASKS * ROW_BLOCK, received.shape[2])
        for row in range(first_row, first_row + rows, ROW_BLOCK)
    ]
    side = jnp.concatenate(sides, axis=1)
    return lax.dot_general(
        side, side, (((1,), (1,)), ((), ())), preferred_element_type=jnp.float32
    )


def fold_gram(blocks):
    size = TASKS * ROW_BLOCK
    row = lax.broadcasted_iota(jnp.int32, (size, size), 0)
    column = lax.broadcasted_iota(jnp.int32, (size, size), 1)
    same = (row % ROW_BLOCK) == (column % ROW_BLOCK)
    task_of = lax.broadcasted_iota(jnp.int32, (size, LANES), 0) // ROW_BLOCK
    lane = lax.broadcasted_iota(jnp.int32, (size, LANES), 1)
    gram = None
    for group, block in enumerate(blocks):
        kept = jnp.where(same, block, 0.0)
        rows_done = jnp.sum(kept.reshape(TASKS, ROW_BLOCK, size), axis=1)
        place = jnp.where(lane == task_of + group * TASKS, 1.0, 0.0)
        part = jnp.dot(
            rows_done, place, precision=lax.Precision.HIGHEST, preferred_element_type=jnp.float32
        )
        gram = part if gram is None else gram + part
    return gram[0:8] + pltpu.roll(gram[8:16], 2 * TASKS, 1)


def exchange_kernel(
    first_ref,
    second_ref,
    first_out,
    second_out,
    gram_out,
    parts,
    slots_y,
    slots_z,
    slots_x,
    piece_send,
    piece_recv,
    stage_send,
    stage_recv,
):
    task = lax.axis_index("task")
    fsdp = lax.axis_index("fsdp")
    chip_x, core = task // CORES, task % CORES
    chip_z, chip_y = fsdp // CHIPS_Y, fsdp % CHIPS_Y
    peers_x = [(lax.rem(task + k, CORES * CHIPS_X), fsdp) for k in range(1, CORES * CHIPS_X)]
    peers_y = [(task, chip_z * CHIPS_Y + lax.rem(chip_y + k, CHIPS_Y)) for k in range(1, CHIPS_Y)]
    peers_z = [(task, lax.rem(chip_z + k, CHIPS_Z) * CHIPS_Y + chip_y) for k in range(1, CHIPS_Z)]

    barrier = pltpu.get_barrier_semaphore()
    everyone = peers_x + peers_y + peers_z
    for peer in everyone:
        pl.semaphore_signal(barrier, inc=1, device_id=peer, device_id_type=MESH)
    pl.semaphore_wait(barrier, len(everyone))

    sources = (first_ref, second_ref)
    received = (first_out, second_out)
    width = first_out.shape[2]
    held = first_ref.shape[0]

    order = []
    for step in (2, 1, 3):
        for other in range(CORES):
            order.append(lax.rem(chip_x + step, CHIPS_X) * CORES + lax.rem(core + other, CORES))
    order.append(chip_x * CORES + (1 - core))

    for index, (group, row, rows) in enumerate(PIECES):
        landing = received[group].at[pl.ds(task * held, held), pl.ds(row, rows), :]
        for target in order:
            columns = pl.ds(pl.multiple_of(target * width, width), width)
            pltpu.make_async_remote_copy(
                src_ref=sources[group].at[:, pl.ds(row, rows), columns],
                dst_ref=landing,
                send_sem=piece_send.at[index],
                recv_sem=piece_recv.at[index],
                device_id=(target, fsdp),
                device_id_type=MESH,
            ).start()
        columns = pl.ds(pl.multiple_of(task * width, width), width)
        pltpu.make_async_copy(
            sources[group].at[:, pl.ds(row, rows), columns], landing, piece_recv.at[index]
        ).start()

    blocks = [None, None]
    for index, (group, row, rows) in enumerate(PIECES):
        whole = received[group].at[:, pl.ds(row, rows), :]
        pltpu.make_async_copy(whole, whole, piece_recv.at[index]).wait()
        block = gram_block(received[group], row, rows)
        blocks[group] = block if blocks[group] is None else blocks[group] + block
    total = fold_gram(blocks)

    stages = (
        (peers_y, chip_y, slots_y),
        (peers_z, chip_z, slots_z),
        (peers_x, task, slots_x),
    )
    for stage, (peers, mine, slots) in enumerate(stages):
        parts[stage] = total
        for peer in peers:
            pltpu.make_async_remote_copy(
                src_ref=parts.at[stage],
                dst_ref=slots.at[mine],
                send_sem=stage_send.at[stage],
                recv_sem=stage_recv.at[stage],
                device_id=peer,
                device_id_type=MESH,
            ).start()
        slots[mine] = total
        arrived = slots.at[pl.ds(0, len(peers))]
        pltpu.make_async_copy(arrived, arrived, stage_recv.at[stage]).wait()
        total = slots[0]
        for member in range(1, len(peers) + 1):
            total = total + slots[member]
    gram_out[...] = total

    for index, (group, row, rows) in enumerate(PIECES):
        sent = received[group].at[pl.ds(0, len(order) * held), pl.ds(row, rows), :]
        pltpu.make_async_copy(sent, sent, piece_send.at[index]).wait()
    for stage, (peers, mine, slots) in enumerate(stages):
        sent = slots.at[pl.ds(0, len(peers))]
        pltpu.make_async_copy(sent, sent, stage_send.at[stage]).wait()


def frank_wolfe(gram):
    lane = lax.broadcasted_iota(jnp.int32, (8, LANES), 1)
    is_first = lane < LANES // 2

    def spread(at):
        return jnp.broadcast_to(gram[:, at : at + 1], (8, LANES))

    columns = []
    for task in range(TASKS):
        upper = jnp.where(is_first, spread(task), spread(TASKS + task))
        lower = jnp.where(is_first, spread(2 * TASKS + task), spread(3 * TASKS + task))
        columns.append((upper, lower))

    def row_of(pair, task):
        return jnp.broadcast_to(pair[task // 8][task % 8 : task % 8 + 1, :], (8, LANES))

    def tree(terms, combine):
        while len(terms) > 1:
            paired = [combine(terms[i], terms[i + 1]) for i in range(0, len(terms) - 1, 2)]
            terms = paired + terms[len(paired) * 2 :]
        return terms[0]

    largest = tree([row_of(columns[task], task) for task in range(TASKS)], jnp.maximum)
    steep = [tuple((part / largest) * (-2.0 / temper) for part in pair) for pair in columns]

    start = jnp.full((8, LANES), 1.0 / TASKS, jnp.float32)
    slope = [tree([steep[task][half] * (1.0 / TASKS) for task in range(TASKS)], jnp.add) for half in range(2)]
    mixture = [start, start]
    for iteration in range(ITERS):
        step = 2.0 / (iteration + 2.0)
        weight = [jnp.exp(half) for half in slope]
        rows = [row_of(weight, task) for task in range(TASKS)]
        scale = step / tree(rows, jnp.add)
        moved = [tree([steep[task][half] * rows[task] for task in range(TASKS)], jnp.add) for half in range(2)]
        slope = [(1.0 - step) * slope[half] + scale * moved[half] for half in range(2)]
        mixture = [(1.0 - step) * mixture[half] + scale * weight[half] for half in range(2)]
    return mixture


UPDATE_ROWS = 32


def update_kernel(
    gram_ref,
    first_ref,
    second_ref,
    first_w,
    first_m,
    first_v,
    second_w,
    second_m,
    second_v,
    out_first_c,
    out_first_w,
    out_first_m,
    out_first_v,
    out_second_c,
    out_second_w,
    out_second_m,
    out_second_v,
    state,
    result,
    mixes,
    in_sem,
    out_sem,
):
    stored = ((first_w, first_m, first_v), (second_w, second_m, second_v))
    outputs = (
        (out_first_c, out_first_w, out_first_m, out_first_v),
        (out_second_c, out_second_w, out_second_m, out_second_v),
    )
    loads = []
    for group in range(2):
        for kind in range(3):
            copy = pltpu.make_async_copy(
                stored[group][kind], state.at[group, kind], in_sem.at[group, kind]
            )
            copy.start()
            loads.append(copy)

    mixture = frank_wolfe(gram_ref[...])
    for half in range(2):
        mixes[8 * half : 8 * half + 8, :] = mixture[half]

    for copy in loads:
        copy.wait()

    rows_all, width = state.shape[2], state.shape[3]
    retained = (first_ref, second_ref)
    stores = []
    for group in range(2):
        lanes = slice(group * (LANES // 2), group * (LANES // 2) + 1)
        weights_of = [
            jnp.broadcast_to(mixes[task : task + 1, lanes], (1, width)) for task in range(TASKS)
        ]
        for block in range(rows_all // UPDATE_ROWS):
            rows = slice(block * UPDATE_ROWS, (block + 1) * UPDATE_ROWS)
            combined = None
            for task in range(TASKS):
                term = weights_of[task] * retained[group][task, rows, :].astype(jnp.float32)
                combined = term if combined is None else combined + term
            weights = state[group, 0, rows, :]
            moment = state[group, 1, rows, :]
            variance = state[group, 2, rows, :]
            new_moment = beta_one * moment + (1.0 - beta_one) * combined
            new_variance = beta_two * variance + (1.0 - beta_two) * combined * combined
            corrected = new_moment / (1.0 - beta_one**adam_step)
            scaled_var = new_variance / (1.0 - beta_two**adam_step)
            new_weights = weights - learn_rate * corrected / (jnp.sqrt(scaled_var) + epsilon)
            values = (combined, new_weights, new_moment, new_variance)
            for kind, value in enumerate(values):
                result[group, kind, rows, :] = value
                copy = pltpu.make_async_copy(
                    result.at[group, kind, rows, :],
                    outputs[group][kind].at[rows, :],
                    out_sem.at[group, block, kind],
                )
                copy.start()
                stores.append(copy)
    for copy in stores:
        copy.wait()


def local(
    grads_first,
    weights_first,
    moment_first,
    variance_first,
    grads_second,
    weights_second,
    moment_second,
    variance_second,
):
    held, rows, columns = grads_first.shape
    width = weights_first.shape[1]
    any_space = pl.BlockSpec(memory_space=pl.ANY)
    in_vmem = pl.BlockSpec(memory_space=pltpu.VMEM)
    in_hbm = pl.BlockSpec(memory_space=pltpu.HBM)
    tile = (8, LANES)
    first, second, gram = pl.pallas_call(
        exchange_kernel,
        name="exchange",
        out_shape=(
            pltpu.VMEM((TASKS, rows, width), jnp.bfloat16),
            pltpu.VMEM((TASKS, rows, width), jnp.bfloat16),
            pltpu.VMEM(tile, jnp.float32),
        ),
        in_specs=[in_hbm, in_hbm],
        out_specs=(in_vmem, in_vmem, in_vmem),
        scratch_shapes=[
            pltpu.VMEM((3,) + tile, jnp.float32),
            pltpu.VMEM((CHIPS_Y,) + tile, jnp.float32),
            pltpu.VMEM((CHIPS_Z,) + tile, jnp.float32),
            pltpu.VMEM((CORES * CHIPS_X,) + tile, jnp.float32),
            pltpu.SemaphoreType.DMA((len(PIECES),)),
            pltpu.SemaphoreType.DMA((len(PIECES),)),
            pltpu.SemaphoreType.DMA((3,)),
            pltpu.SemaphoreType.DMA((3,)),
        ],
        compiler_params=pltpu.CompilerParams(
            collective_id=0, has_side_effects=True, vmem_limit_bytes=32 * 1024 * 1024
        ),
    )(grads_first, grads_second)

    shape = jax.ShapeDtypeStruct((rows, width), jnp.float32)
    return pl.pallas_call(
        update_kernel,
        name="update",
        out_shape=(shape,) * 8,
        in_specs=[in_vmem] * 3 + [any_space] * 6,
        out_specs=(in_hbm,) * 8,
        scratch_shapes=[
            pltpu.VMEM((2, 3, rows, width), jnp.float32),
            pltpu.VMEM((2, 4, rows, width), jnp.float32),
            pltpu.VMEM((TASKS, LANES), jnp.float32),
            pltpu.SemaphoreType.DMA((2, 3)),
            pltpu.SemaphoreType.DMA((2, rows // UPDATE_ROWS, 4)),
        ],
        compiler_params=pltpu.CompilerParams(vmem_limit_bytes=32 * 1024 * 1024),
    )(
        gram,
        first,
        second,
        weights_first,
        moment_first,
        variance_first,
        weights_second,
        moment_second,
        variance_second,
    )


def solution(mesh):
    in_specs = (
        P("task", "fsdp", None),
        P("fsdp", "task"),
        P("fsdp", "task"),
        P("fsdp", "task"),
        P("task", "fsdp", None),
        P("fsdp", "task"),
        P("fsdp", "task"),
        P("fsdp", "task"),
    )
    out_specs = (P("fsdp", "task"),) * 8
    return jax.shard_map(local, mesh=mesh, in_specs=in_specs, out_specs=out_specs, check_vma=False)
```

```python
import functools

import jax
import jax.numpy as jnp
from jax import lax
from jax.experimental import pallas as pl
from jax.experimental.pallas import tpu as pltpu
from jax.sharding import PartitionSpec as P

ITERS = 20

temper = 0.05
beta_one = 0.9
beta_two = 0.999
learn_rate = 0.001
adam_step = 1000.0
epsilon = 1e-08

MESH = pl.DeviceIdType.MESH
TASKS = 16
CORES = 2
CHIPS_X = 4
CHIPS_Y = 4
CHIPS_Z = 8
LANES = 128
ROW_BLOCK = 16
PIECES = ((0, 0, 128), (1, 0, 96), (1, 96, 32))


def gram_block(received, first_row, rows):
    sides = [
        received[:, row : row + ROW_BLOCK, :].reshape(TASKS * ROW_BLOCK, received.shape[2])
        for row in range(first_row, first_row + rows, ROW_BLOCK)
    ]
    side = jnp.concatenate(sides, axis=1)
    return lax.dot_general(
        side, side, (((1,), (1,)), ((), ())), preferred_element_type=jnp.float32
    )


def fold_gram(blocks):
    size = TASKS * ROW_BLOCK
    row = lax.broadcasted_iota(jnp.int32, (size, size), 0)
    column = lax.broadcasted_iota(jnp.int32, (size, size), 1)
    same = (row % ROW_BLOCK) == (column % ROW_BLOCK)
    task_of = lax.broadcasted_iota(jnp.int32, (size, LANES), 0) // ROW_BLOCK
    lane = lax.broadcasted_iota(jnp.int32, (size, LANES), 1)
    gram = None
    for group, block in enumerate(blocks):
        kept = jnp.where(same, block, 0.0)
        rows_done = jnp.sum(kept.reshape(TASKS, ROW_BLOCK, size), axis=1)
        place = jnp.where(lane == task_of + group * TASKS, 1.0, 0.0)
        part = jnp.dot(
            rows_done, place, precision=lax.Precision.HIGHEST, preferred_element_type=jnp.float32
        )
        gram = part if gram is None else gram + part
    half = gram[0:8] + pltpu.roll(gram[8:16], 2 * TASKS, 1)
    return (half + pltpu.roll(pltpu.roll(half, LANES // 2, 1), 4, 0))[0:4]


def tree(terms, combine):
    while len(terms) > 1:
        paired = [combine(terms[i], terms[i + 1]) for i in range(0, len(terms) - 1, 2)]
        terms = paired + terms[len(paired) * 2 :]
    return terms[0]


def exchange_kernel(
    first_ref,
    second_ref,
    first_out,
    second_out,
    gram_out,
    parts,
    slots_plane,
    slots_z,
    piece_send,
    piece_recv,
    stage_send,
    stage_recv,
    entered,
):
    task = lax.axis_index("task")
    fsdp = lax.axis_index("fsdp")
    chip_x, core = task // CORES, task % CORES
    chip_z, chip_y = fsdp // CHIPS_Y, fsdp % CHIPS_Y
    peers_x = [(lax.rem(task + k, CORES * CHIPS_X), fsdp) for k in range(1, CORES * CHIPS_X)]
    peers_y = [(task, chip_z * CHIPS_Y + lax.rem(chip_y + k, CHIPS_Y)) for k in range(1, CHIPS_Y)]
    peers_z = [(task, lax.rem(chip_z + k, CHIPS_Z) * CHIPS_Y + chip_y) for k in range(1, CHIPS_Z)]

    peers_plane = [
        (lax.rem(task + other, CORES * CHIPS_X), chip_z * CHIPS_Y + lax.rem(chip_y + step, CHIPS_Y))
        for step in (2, 1, 3, 0)
        for other in (4, 5, 3, 2, 6, 7, 1, 0)
        if (step, other) != (0, 0)
    ]
    beside_z = [peers_z[0], peers_z[-1]]

    barrier = pltpu.get_barrier_semaphore()
    near = peers_x + peers_y + beside_z
    for peer in near:
        pl.semaphore_signal(barrier, inc=1, device_id=peer, device_id_type=MESH)
    pl.semaphore_wait(barrier, len(near))

    sources = (first_ref, second_ref)
    received = (first_out, second_out)
    width = first_out.shape[2]
    held = first_ref.shape[0]

    order = []
    for step in (2, 1, 3):
        for other in range(CORES):
            order.append(lax.rem(chip_x + step, CHIPS_X) * CORES + lax.rem(core + other, CORES))
    order.append(chip_x * CORES + (1 - core))

    for index, (group, row, rows) in enumerate(PIECES):
        landing = received[group].at[pl.ds(task * held, held), pl.ds(row, rows), :]
        for target in order:
            columns = pl.ds(pl.multiple_of(target * width, width), width)
            pltpu.make_async_remote_copy(
                src_ref=sources[group].at[:, pl.ds(row, rows), columns],
                dst_ref=landing,
                send_sem=piece_send.at[index],
                recv_sem=piece_recv.at[index],
                device_id=(target, fsdp),
                device_id_type=MESH,
            ).start()
        columns = pl.ds(pl.multiple_of(task * width, width), width)
        pltpu.make_async_copy(
            sources[group].at[:, pl.ds(row, rows), columns], landing, piece_recv.at[index]
        ).start()

    for turn, tellers in enumerate((peers_y, beside_z, beside_z, beside_z)):
        for peer in tellers:
            pl.semaphore_signal(entered.at[turn], inc=1, device_id=peer, device_id_type=MESH)
        pl.semaphore_wait(entered.at[turn], len(tellers))

    blocks = [None, None]
    for index, (group, row, rows) in enumerate(PIECES):
        whole = received[group].at[:, pl.ds(row, rows), :]
        pltpu.make_async_copy(whole, whole, piece_recv.at[index]).wait()
        block = gram_block(received[group], row, rows)
        blocks[group] = block if blocks[group] is None else blocks[group] + block
    total = fold_gram(blocks)

    stages = (
        (peers_plane, chip_y * CORES * CHIPS_X + task, slots_plane),
        (peers_z, chip_z, slots_z),
    )
    for stage, (peers, mine, slots) in enumerate(stages):
        parts[stage] = total
        for peer in peers:
            pltpu.make_async_remote_copy(
                src_ref=parts.at[stage],
                dst_ref=slots.at[mine],
                send_sem=stage_send.at[stage],
                recv_sem=stage_recv.at[stage],
                device_id=peer,
                device_id_type=MESH,
            ).start()
        slots[mine] = total
        arrived = slots.at[pl.ds(0, len(peers))]
        pltpu.make_async_copy(arrived, arrived, stage_recv.at[stage]).wait()
        total = tree([slots[member] for member in range(len(peers) + 1)], jnp.add)
    gram_out[0:4, :] = total
    gram_out[4:8, :] = pltpu.roll(total, LANES // 2, 1)

    for index, (group, row, rows) in enumerate(PIECES):
        sent = received[group].at[pl.ds(0, len(order) * held), pl.ds(row, rows), :]
        pltpu.make_async_copy(sent, sent, piece_send.at[index]).wait()
    for stage, (peers, mine, slots) in enumerate(stages):
        sent = slots.at[pl.ds(0, len(peers))]
        pltpu.make_async_copy(sent, sent, stage_send.at[stage]).wait()


def frank_wolfe(gram):
    lane = lax.broadcasted_iota(jnp.int32, (8, LANES), 1)
    is_first = lane < LANES // 2

    def spread(at):
        return jnp.broadcast_to(gram[:, at : at + 1], (8, LANES))

    columns = []
    for task in range(TASKS):
        upper = jnp.where(is_first, spread(task), spread(TASKS + task))
        lower = jnp.where(is_first, spread(2 * TASKS + task), spread(3 * TASKS + task))
        columns.append((upper, lower))

    def row_of(pair, task):
        return jnp.broadcast_to(pair[task // 8][task % 8 : task % 8 + 1, :], (8, LANES))

    largest = tree([row_of(columns[task], task) for task in range(TASKS)], jnp.maximum)
    steep = [tuple((part / largest) * (-2.0 / temper) for part in pair) for pair in columns]

    start = jnp.full((8, LANES), 1.0 / TASKS, jnp.float32)
    slope = [tree([steep[task][half] * (1.0 / TASKS) for task in range(TASKS)], jnp.add) for half in range(2)]
    mixture = [start, start]
    for iteration in range(ITERS):
        step = 2.0 / (iteration + 2.0)
        weight = [jnp.exp(half) for half in slope]
        rows = [row_of(weight, task) for task in range(TASKS)]
        scale = step / tree(rows, jnp.add)
        moved = [tree([steep[task][half] * rows[task] for task in range(TASKS)], jnp.add) for half in range(2)]
        slope = [(1.0 - step) * slope[half] + scale * moved[half] for half in range(2)]
        mixture = [(1.0 - step) * mixture[half] + scale * weight[half] for half in range(2)]
    return mixture


UPDATE_ROWS = 32


def update_kernel(
    gram_ref,
    first_ref,
    second_ref,
    first_w,
    first_m,
    first_v,
    second_w,
    second_m,
    second_v,
    out_first_c,
    out_first_w,
    out_first_m,
    out_first_v,
    out_second_c,
    out_second_w,
    out_second_m,
    out_second_v,
    state,
    result,
    mixes,
    in_sem,
    out_sem,
):
    stored = ((first_w, first_m, first_v), (second_w, second_m, second_v))
    outputs = (
        (out_first_c, out_first_w, out_first_m, out_first_v),
        (out_second_c, out_second_w, out_second_m, out_second_v),
    )
    loads = []
    for group in range(2):
        for kind in range(3):
            copy = pltpu.make_async_copy(
                stored[group][kind], state.at[group, kind], in_sem.at[group, kind]
            )
            copy.start()
            loads.append(copy)

    mixture = frank_wolfe(gram_ref[...])
    for half in range(2):
        mixes[8 * half : 8 * half + 8, :] = mixture[half]

    for copy in loads:
        copy.wait()

    rows_all, width = state.shape[2], state.shape[3]
    retained = (first_ref, second_ref)
    stores = []
    for group in range(2):
        lanes = slice(group * (LANES // 2), group * (LANES // 2) + 1)
        weights_of = [
            jnp.broadcast_to(mixes[task : task + 1, lanes], (1, width)) for task in range(TASKS)
        ]
        for block in range(rows_all // UPDATE_ROWS):
            rows = slice(block * UPDATE_ROWS, (block + 1) * UPDATE_ROWS)
            combined = None
            for task in range(TASKS):
                term = weights_of[task] * retained[group][task, rows, :].astype(jnp.float32)
                combined = term if combined is None else combined + term
            weights = state[group, 0, rows, :]
            moment = state[group, 1, rows, :]
            variance = state[group, 2, rows, :]
            new_moment = beta_one * moment + (1.0 - beta_one) * combined
            new_variance = beta_two * variance + (1.0 - beta_two) * combined * combined
            corrected = new_moment / (1.0 - beta_one**adam_step)
            scaled_var = new_variance / (1.0 - beta_two**adam_step)
            new_weights = weights - learn_rate * corrected / (jnp.sqrt(scaled_var) + epsilon)
            values = (combined, new_weights, new_moment, new_variance)
            for kind, value in enumerate(values):
                result[group, kind, rows, :] = value
                copy = pltpu.make_async_copy(
                    result.at[group, kind, rows, :],
                    outputs[group][kind].at[rows, :],
                    out_sem.at[group, block, kind],
                )
                copy.start()
                stores.append(copy)
    for copy in stores:
        copy.wait()


def local(
    grads_first,
    weights_first,
    moment_first,
    variance_first,
    grads_second,
    weights_second,
    moment_second,
    variance_second,
):
    held, rows, columns = grads_first.shape
    width = weights_first.shape[1]
    any_space = pl.BlockSpec(memory_space=pl.ANY)
    in_vmem = pl.BlockSpec(memory_space=pltpu.VMEM)
    in_hbm = pl.BlockSpec(memory_space=pltpu.HBM)
    tile = (8, LANES)
    packed = (4, LANES)
    first, second, gram = pl.pallas_call(
        exchange_kernel,
        name="exchange",
        out_shape=(
            pltpu.VMEM((TASKS, rows, width), jnp.bfloat16),
            pltpu.VMEM((TASKS, rows, width), jnp.bfloat16),
            pltpu.VMEM(tile, jnp.float32),
        ),
        in_specs=[in_hbm, in_hbm],
        out_specs=(in_vmem, in_vmem, in_vmem),
        scratch_shapes=[
            pltpu.VMEM((2,) + packed, jnp.float32),
            pltpu.VMEM((CHIPS_Y * CHIPS_X * CORES,) + packed, jnp.float32),
            pltpu.VMEM((CHIPS_Z,) + packed, jnp.float32),
            pltpu.SemaphoreType.DMA((len(PIECES),)),
            pltpu.SemaphoreType.DMA((len(PIECES),)),
            pltpu.SemaphoreType.DMA((2,)),
            pltpu.SemaphoreType.DMA((2,)),
            pltpu.SemaphoreType.REGULAR((4,)),
        ],
        compiler_params=pltpu.CompilerParams(
            collective_id=0, has_side_effects=True, vmem_limit_bytes=60 * 1000 * 1000
        ),
    )(grads_first, grads_second)

    shape = jax.ShapeDtypeStruct((rows, width), jnp.float32)
    return pl.pallas_call(
        update_kernel,
        name="update",
        out_shape=(shape,) * 8,
        in_specs=[in_vmem] * 3 + [any_space] * 6,
        out_specs=(in_hbm,) * 8,
        scratch_shapes=[
            pltpu.VMEM((2, 3, rows, width), jnp.float32),
            pltpu.VMEM((2, 4, rows, width), jnp.float32),
            pltpu.VMEM((TASKS, LANES), jnp.float32),
            pltpu.SemaphoreType.DMA((2, 3)),
            pltpu.SemaphoreType.DMA((2, rows // UPDATE_ROWS, 4)),
        ],
        compiler_params=pltpu.CompilerParams(vmem_limit_bytes=32 * 1024 * 1024),
    )(
        gram,
        first,
        second,
        weights_first,
        moment_first,
        variance_first,
        weights_second,
        moment_second,
        variance_second,
    )


def solution(mesh):
    in_specs = (
        P("task", "fsdp", None),
        P("fsdp", "task"),
        P("fsdp", "task"),
        P("fsdp", "task"),
        P("task", "fsdp", None),
        P("fsdp", "task"),
        P("fsdp", "task"),
        P("fsdp", "task"),
    )
    out_specs = (P("fsdp", "task"),) * 8
    return jax.shard_map(local, mesh=mesh, in_specs=in_specs, out_specs=out_specs, check_vma=False)
```

```python
import jax
import jax.numpy as jnp
from jax import lax
from jax.experimental import pallas as pl
from jax.experimental.pallas import tpu as pltpu
from jax.sharding import PartitionSpec as P

ITERS = 20

temper = 0.05
beta_one = 0.9
beta_two = 0.999
learn_rate = 0.001
adam_step = 1000.0
epsilon = 1e-08

MESH = pl.DeviceIdType.MESH
TASKS = 16
CORES = 2
CHIPS_X = 4
CHIPS_Y = 4
CHIPS_Z = 8
LANES = 128
ROW_BLOCK = 16
PIECES = ((0, 0, 128), (1, 0, 64), (1, 64, 48), (1, 112, 16))


def gram_block(received, first_row, rows):
    sides = [
        received[:, row : row + ROW_BLOCK, :].reshape(TASKS * ROW_BLOCK, received.shape[2])
        for row in range(first_row, first_row + rows, ROW_BLOCK)
    ]
    side = jnp.concatenate(sides, axis=1)
    return lax.dot_general(
        side, side, (((1,), (1,)), ((), ())), preferred_element_type=jnp.float32
    )


def fold_gram(group, block):
    size = TASKS * ROW_BLOCK
    row = lax.broadcasted_iota(jnp.int32, (size, size), 0)
    column = lax.broadcasted_iota(jnp.int32, (size, size), 1)
    same = (row % ROW_BLOCK) == (column % ROW_BLOCK)
    task_of = lax.broadcasted_iota(jnp.int32, (size, LANES), 0) // ROW_BLOCK
    lane = lax.broadcasted_iota(jnp.int32, (size, LANES), 1)
    kept = jnp.where(same, block, 0.0)
    rows_done = jnp.sum(kept.reshape(TASKS, ROW_BLOCK, size), axis=1)
    place = jnp.where(lane == task_of + group * TASKS, 1.0, 0.0)
    gram = jnp.dot(
        rows_done, place, precision=lax.Precision.HIGHEST, preferred_element_type=jnp.float32
    )
    half = gram[0:8] + pltpu.roll(gram[8:16], 2 * TASKS, 1)
    return (half + pltpu.roll(pltpu.roll(half, LANES // 2, 1), 4, 0))[0:4]


def tree(terms, combine):
    while len(terms) > 1:
        paired = [combine(terms[i], terms[i + 1]) for i in range(0, len(terms) - 1, 2)]
        terms = paired + terms[len(paired) * 2 :]
    return terms[0]


def exchange_kernel(
    first_ref,
    second_ref,
    first_out,
    second_out,
    gram_out,
    parts,
    slots_plane,
    slots_z,
    piece_send,
    piece_recv,
    stage_send,
    stage_recv,
    entered,
):
    task = lax.axis_index("task")
    fsdp = lax.axis_index("fsdp")
    chip_x, core = task // CORES, task % CORES
    chip_z, chip_y = fsdp // CHIPS_Y, fsdp % CHIPS_Y
    peers_x = [(lax.rem(task + k, CORES * CHIPS_X), fsdp) for k in range(1, CORES * CHIPS_X)]
    peers_y = [(task, chip_z * CHIPS_Y + lax.rem(chip_y + k, CHIPS_Y)) for k in range(1, CHIPS_Y)]
    peers_z = [(task, lax.rem(chip_z + k, CHIPS_Z) * CHIPS_Y + chip_y) for k in range(1, CHIPS_Z)]

    peers_plane = [
        (lax.rem(task + other, CORES * CHIPS_X), chip_z * CHIPS_Y + lax.rem(chip_y + step, CHIPS_Y))
        for step in (2, 1, 3, 0)
        for other in (4, 5, 3, 2, 6, 7, 1, 0)
        if (step, other) != (0, 0)
    ]
    beside_z = [peers_z[0], peers_z[-1]]

    barrier = pltpu.get_barrier_semaphore()
    near = peers_x + peers_y + beside_z
    for peer in near:
        pl.semaphore_signal(barrier, inc=1, device_id=peer, device_id_type=MESH)
    pl.semaphore_wait(barrier, len(near))

    sources = (first_ref, second_ref)
    received = (first_out, second_out)
    width = first_out.shape[2]
    held = first_ref.shape[0]

    order = []
    for step in (2, 1, 3):
        for other in range(CORES):
            order.append(lax.rem(chip_x + step, CHIPS_X) * CORES + lax.rem(core + other, CORES))
    order.append(chip_x * CORES + (1 - core))

    for index, (group, row, rows) in enumerate(PIECES):
        landing = received[group].at[pl.ds(task * held, held), pl.ds(row, rows), :]
        for target in order:
            columns = pl.ds(pl.multiple_of(target * width, width), width)
            pltpu.make_async_remote_copy(
                src_ref=sources[group].at[:, pl.ds(row, rows), columns],
                dst_ref=landing,
                send_sem=piece_send.at[index],
                recv_sem=piece_recv.at[index],
                device_id=(target, fsdp),
                device_id_type=MESH,
            ).start()
        columns = pl.ds(pl.multiple_of(task * width, width), width)
        pltpu.make_async_copy(
            sources[group].at[:, pl.ds(row, rows), columns], landing, piece_recv.at[index]
        ).start()

    for turn, tellers in enumerate((peers_y, beside_z, beside_z, beside_z)):
        for peer in tellers:
            pl.semaphore_signal(entered.at[turn], inc=1, device_id=peer, device_id_type=MESH)
        pl.semaphore_wait(entered.at[turn], len(tellers))

    total = None
    for index, (group, row, rows) in enumerate(PIECES):
        whole = received[group].at[:, pl.ds(row, rows), :]
        pltpu.make_async_copy(whole, whole, piece_recv.at[index]).wait()
        part = fold_gram(group, gram_block(received[group], row, rows))
        total = part if total is None else total + part

    stages = (
        (peers_plane, chip_y * CORES * CHIPS_X + task, slots_plane),
        (peers_z, chip_z, slots_z),
    )
    for stage, (peers, mine, slots) in enumerate(stages):
        parts[stage] = total
        for peer in peers:
            pltpu.make_async_remote_copy(
                src_ref=parts.at[stage],
                dst_ref=slots.at[mine],
                send_sem=stage_send.at[stage],
                recv_sem=stage_recv.at[stage],
                device_id=peer,
                device_id_type=MESH,
            ).start()
        slots[mine] = total
        arrived = slots.at[pl.ds(0, len(peers))]
        pltpu.make_async_copy(arrived, arrived, stage_recv.at[stage]).wait()
        total = tree([slots[member] for member in range(len(peers) + 1)], jnp.add)
    gram_out[0:4, :] = total
    gram_out[4:8, :] = pltpu.roll(total, LANES // 2, 1)

    for index, (group, row, rows) in enumerate(PIECES):
        sent = received[group].at[pl.ds(0, len(order) * held), pl.ds(row, rows), :]
        pltpu.make_async_copy(sent, sent, piece_send.at[index]).wait()
    for stage, (peers, mine, slots) in enumerate(stages):
        sent = slots.at[pl.ds(0, len(peers))]
        pltpu.make_async_copy(sent, sent, stage_send.at[stage]).wait()


def frank_wolfe(gram):
    lane = lax.broadcasted_iota(jnp.int32, (8, LANES), 1)
    is_first = lane < LANES // 2

    def spread(at):
        return jnp.broadcast_to(gram[:, at : at + 1], (8, LANES))

    columns = []
    for task in range(TASKS):
        upper = jnp.where(is_first, spread(task), spread(TASKS + task))
        lower = jnp.where(is_first, spread(2 * TASKS + task), spread(3 * TASKS + task))
        columns.append((upper, lower))

    def row_of(pair, task):
        return jnp.broadcast_to(pair[task // 8][task % 8 : task % 8 + 1, :], (8, LANES))

    largest = tree([row_of(columns[task], task) for task in range(TASKS)], jnp.maximum)
    steep = [tuple((part / largest) * (-2.0 / temper) for part in pair) for pair in columns]

    start = jnp.full((8, LANES), 1.0 / TASKS, jnp.float32)
    slope = [tree([steep[task][half] * (1.0 / TASKS) for task in range(TASKS)], jnp.add) for half in range(2)]
    mixture = [start, start]
    for iteration in range(ITERS):
        step = 2.0 / (iteration + 2.0)
        weight = [jnp.exp(half) for half in slope]
        rows = [row_of(weight, task) for task in range(TASKS)]
        scale = step / tree(rows, jnp.add)
        moved = [tree([steep[task][half] * rows[task] for task in range(TASKS)], jnp.add) for half in range(2)]
        slope = [(1.0 - step) * slope[half] + scale * moved[half] for half in range(2)]
        mixture = [(1.0 - step) * mixture[half] + scale * weight[half] for half in range(2)]
    return mixture


UPDATE_ROWS = 32


def update_kernel(
    gram_ref,
    first_ref,
    second_ref,
    first_w,
    first_m,
    first_v,
    second_w,
    second_m,
    second_v,
    out_first_c,
    out_first_w,
    out_first_m,
    out_first_v,
    out_second_c,
    out_second_w,
    out_second_m,
    out_second_v,
    result,
    mixes,
    out_sem,
):
    stored = ((first_w, first_m, first_v), (second_w, second_m, second_v))
    outputs = (
        (out_first_c, out_first_w, out_first_m, out_first_v),
        (out_second_c, out_second_w, out_second_m, out_second_v),
    )
    mixture = frank_wolfe(gram_ref[...])
    for half in range(2):
        mixes[8 * half : 8 * half + 8, :] = mixture[half]

    rows_all, width = first_w.shape
    retained = (first_ref, second_ref)
    stores = []
    for group in range(2):
        lanes = slice(group * (LANES // 2), group * (LANES // 2) + 1)
        weights_of = [
            jnp.broadcast_to(mixes[task : task + 1, lanes], (1, width)) for task in range(TASKS)
        ]
        for block in range(rows_all // UPDATE_ROWS):
            rows = slice(block * UPDATE_ROWS, (block + 1) * UPDATE_ROWS)
            combined = None
            for task in range(TASKS):
                term = weights_of[task] * retained[group][task, rows, :].astype(jnp.float32)
                combined = term if combined is None else combined + term
            weights = stored[group][0][rows, :]
            moment = stored[group][1][rows, :]
            variance = stored[group][2][rows, :]
            new_moment = beta_one * moment + (1.0 - beta_one) * combined
            new_variance = beta_two * variance + (1.0 - beta_two) * combined * combined
            moved = new_moment * (learn_rate / (1.0 - beta_one**adam_step))
            scaled_var = new_variance * (1.0 / (1.0 - beta_two**adam_step))
            new_weights = weights - moved / (jnp.sqrt(scaled_var) + epsilon)
            values = (combined, new_weights, new_moment, new_variance)
            for kind, value in enumerate(values):
                result[group, kind, rows, :] = value
                copy = pltpu.make_async_copy(
                    result.at[group, kind, rows, :],
                    outputs[group][kind].at[rows, :],
                    out_sem.at[group, block, kind],
                )
                copy.start()
                stores.append(copy)
    for copy in stores:
        copy.wait()


def local(
    grads_first,
    weights_first,
    moment_first,
    variance_first,
    grads_second,
    weights_second,
    moment_second,
    variance_second,
):
    held, rows, columns = grads_first.shape
    width = weights_first.shape[1]
    in_vmem = pl.BlockSpec(memory_space=pltpu.VMEM)
    in_hbm = pl.BlockSpec(memory_space=pltpu.HBM)
    tile = (8, LANES)
    packed = (4, LANES)
    first, second, gram = pl.pallas_call(
        exchange_kernel,
        name="exchange",
        out_shape=(
            pltpu.VMEM((TASKS, rows, width), jnp.bfloat16),
            pltpu.VMEM((TASKS, rows, width), jnp.bfloat16),
            pltpu.VMEM(tile, jnp.float32),
        ),
        in_specs=[in_hbm, in_hbm],
        out_specs=(in_vmem, in_vmem, in_vmem),
        scratch_shapes=[
            pltpu.VMEM((2,) + packed, jnp.float32),
            pltpu.VMEM((CHIPS_Y * CHIPS_X * CORES,) + packed, jnp.float32),
            pltpu.VMEM((CHIPS_Z,) + packed, jnp.float32),
            pltpu.SemaphoreType.DMA((len(PIECES),)),
            pltpu.SemaphoreType.DMA((len(PIECES),)),
            pltpu.SemaphoreType.DMA((2,)),
            pltpu.SemaphoreType.DMA((2,)),
            pltpu.SemaphoreType.REGULAR((4,)),
        ],
        compiler_params=pltpu.CompilerParams(
            collective_id=0, has_side_effects=True, vmem_limit_bytes=60 * 1000 * 1000
        ),
    )(grads_first, grads_second)

    shape = jax.ShapeDtypeStruct((rows, width), jnp.float32)
    return pl.pallas_call(
        update_kernel,
        name="update",
        out_shape=(shape,) * 8,
        in_specs=[in_vmem] * 9,
        out_specs=(in_hbm,) * 8,
        scratch_shapes=[
            pltpu.VMEM((2, 4, rows, width), jnp.float32),
            pltpu.VMEM((TASKS, LANES), jnp.float32),
            pltpu.SemaphoreType.DMA((2, rows // UPDATE_ROWS, 4)),
        ],
        compiler_params=pltpu.CompilerParams(vmem_limit_bytes=32 * 1024 * 1024),
    )(
        gram,
        first,
        second,
        weights_first,
        moment_first,
        variance_first,
        weights_second,
        moment_second,
        variance_second,
    )


def solution(mesh):
    in_specs = (
        P("task", "fsdp", None),
        P("fsdp", "task"),
        P("fsdp", "task"),
        P("fsdp", "task"),
        P("task", "fsdp", None),
        P("fsdp", "task"),
        P("fsdp", "task"),
        P("fsdp", "task"),
    )
    out_specs = (P("fsdp", "task"),) * 8
    return jax.shard_map(local, mesh=mesh, in_specs=in_specs, out_specs=out_specs, check_vma=False)
```

```python
import jax
import jax.numpy as jnp
from jax import lax
from jax.experimental import pallas as pl
from jax.experimental.pallas import tpu as pltpu
from jax.sharding import PartitionSpec as P

ITERS = 20

temper = 0.05
beta_one = 0.9
beta_two = 0.999
learn_rate = 0.001
adam_step = 1000.0
epsilon = 1e-08

MESH = pl.DeviceIdType.MESH
TASKS = 16
CORES = 2
CHIPS_X = 4
CHIPS_Y = 4
CHIPS_Z = 8
LANES = 128
ROW_BLOCK = 16
PIECES = ((0, 0, 128), (1, 0, 64), (1, 64, 48), (1, 112, 16))


def gram_block(received, first_row, rows):
    sides = [
        received[:, row : row + ROW_BLOCK, :].reshape(TASKS * ROW_BLOCK, received.shape[2])
        for row in range(first_row, first_row + rows, ROW_BLOCK)
    ]
    side = jnp.concatenate(sides, axis=1)
    return lax.dot_general(
        side, side, (((1,), (1,)), ((), ())), preferred_element_type=jnp.float32
    )


def fold_gram(group, block):
    size = TASKS * ROW_BLOCK
    row = lax.broadcasted_iota(jnp.int32, (size, size), 0)
    column = lax.broadcasted_iota(jnp.int32, (size, size), 1)
    same = (row % ROW_BLOCK) == (column % ROW_BLOCK)
    task_of = lax.broadcasted_iota(jnp.int32, (size, LANES), 0) // ROW_BLOCK
    lane = lax.broadcasted_iota(jnp.int32, (size, LANES), 1)
    kept = jnp.where(same, block, 0.0)
    rows_done = jnp.sum(kept.reshape(TASKS, ROW_BLOCK, size), axis=1)
    place = jnp.where(lane == task_of + group * TASKS, 1.0, 0.0)
    gram = jnp.dot(
        rows_done, place, precision=lax.Precision.HIGHEST, preferred_element_type=jnp.float32
    )
    half = gram[0:8] + pltpu.roll(gram[8:16], 2 * TASKS, 1)
    return (half + pltpu.roll(pltpu.roll(half, LANES // 2, 1), 4, 0))[0:4]


def tree(terms, combine):
    while len(terms) > 1:
        paired = [combine(terms[i], terms[i + 1]) for i in range(0, len(terms) - 1, 2)]
        terms = paired + terms[len(paired) * 2 :]
    return terms[0]


def exchange_kernel(
    first_ref,
    second_ref,
    first_out,
    second_out,
    gram_out,
    parts,
    slots_plane,
    slots_z,
    piece_send,
    piece_recv,
    stage_send,
    stage_recv,
    entered,
):
    task = lax.axis_index("task")
    fsdp = lax.axis_index("fsdp")
    chip_x, core = task // CORES, task % CORES
    chip_z, chip_y = fsdp // CHIPS_Y, fsdp % CHIPS_Y
    peers_x = [(lax.rem(task + k, CORES * CHIPS_X), fsdp) for k in range(1, CORES * CHIPS_X)]
    peers_y = [(task, chip_z * CHIPS_Y + lax.rem(chip_y + k, CHIPS_Y)) for k in range(1, CHIPS_Y)]
    peers_z = [(task, lax.rem(chip_z + k, CHIPS_Z) * CHIPS_Y + chip_y) for k in range(1, CHIPS_Z)]

    peers_plane = [
        (lax.rem(task + other, CORES * CHIPS_X), chip_z * CHIPS_Y + lax.rem(chip_y + step, CHIPS_Y))
        for step in (2, 1, 3, 0)
        for other in (4, 5, 3, 2, 6, 7, 1, 0)
        if (step, other) != (0, 0)
    ]
    beside_z = [peers_z[0], peers_z[-1]]

    barrier = pltpu.get_barrier_semaphore()
    near = peers_x + peers_y + beside_z
    for peer in near:
        pl.semaphore_signal(barrier, inc=1, device_id=peer, device_id_type=MESH)
    pl.semaphore_wait(barrier, len(near))

    sources = (first_ref, second_ref)
    received = (first_out, second_out)
    width = first_out.shape[2]
    held = first_ref.shape[0]

    order = []
    for step in (2, 1, 3):
        for other in range(CORES):
            order.append(lax.rem(chip_x + step, CHIPS_X) * CORES + lax.rem(core + other, CORES))
    order.append(chip_x * CORES + (1 - core))

    for index, (group, row, rows) in enumerate(PIECES):
        landing = received[group].at[pl.ds(task * held, held), pl.ds(row, rows), :]
        for target in order:
            columns = pl.ds(pl.multiple_of(target * width, width), width)
            pltpu.make_async_remote_copy(
                src_ref=sources[group].at[:, pl.ds(row, rows), columns],
                dst_ref=landing,
                send_sem=piece_send.at[index],
                recv_sem=piece_recv.at[index],
                device_id=(target, fsdp),
                device_id_type=MESH,
            ).start()
        columns = pl.ds(pl.multiple_of(task * width, width), width)
        pltpu.make_async_copy(
            sources[group].at[:, pl.ds(row, rows), columns], landing, piece_recv.at[index]
        ).start()

    for turn, tellers in enumerate((peers_y, beside_z, beside_z, beside_z)):
        for peer in tellers:
            pl.semaphore_signal(entered.at[turn], inc=1, device_id=peer, device_id_type=MESH)
        pl.semaphore_wait(entered.at[turn], len(tellers))

    total = None
    for index, (group, row, rows) in enumerate(PIECES):
        whole = received[group].at[:, pl.ds(row, rows), :]
        pltpu.make_async_copy(whole, whole, piece_recv.at[index]).wait()
        part = fold_gram(group, gram_block(received[group], row, rows))
        total = part if total is None else total + part

    stages = (
        (peers_plane, chip_y * CORES * CHIPS_X + task, slots_plane),
        (peers_z, chip_z, slots_z),
    )
    for stage, (peers, mine, slots) in enumerate(stages):
        parts[stage] = total
        for peer in peers:
            pltpu.make_async_remote_copy(
                src_ref=parts.at[stage],
                dst_ref=slots.at[mine],
                send_sem=stage_send.at[stage],
                recv_sem=stage_recv.at[stage],
                device_id=peer,
                device_id_type=MESH,
            ).start()
        slots[mine] = total
        arrived = slots.at[pl.ds(0, len(peers))]
        pltpu.make_async_copy(arrived, arrived, stage_recv.at[stage]).wait()
        total = tree([slots[member] for member in range(len(peers) + 1)], jnp.add)
    gram_out[0:4, :] = total
    gram_out[4:8, :] = pltpu.roll(total, LANES // 2, 1)

    for index, (group, row, rows) in enumerate(PIECES):
        sent = received[group].at[pl.ds(0, len(order) * held), pl.ds(row, rows), :]
        pltpu.make_async_copy(sent, sent, piece_send.at[index]).wait()
    for stage, (peers, mine, slots) in enumerate(stages):
        sent = slots.at[pl.ds(0, len(peers))]
        pltpu.make_async_copy(sent, sent, stage_send.at[stage]).wait()


def frank_wolfe(gram):
    lane = lax.broadcasted_iota(jnp.int32, (8, LANES), 1)
    is_first = lane < LANES // 2

    def spread(at):
        return jnp.broadcast_to(gram[:, at : at + 1], (8, LANES))

    columns = []
    for task in range(TASKS):
        upper = jnp.where(is_first, spread(task), spread(TASKS + task))
        lower = jnp.where(is_first, spread(2 * TASKS + task), spread(3 * TASKS + task))
        columns.append((upper, lower))

    def row_of(pair, task):
        return jnp.broadcast_to(pair[task // 8][task % 8 : task % 8 + 1, :], (8, LANES))

    largest = tree([row_of(columns[task], task) for task in range(TASKS)], jnp.maximum)
    steep = [tuple((part / largest) * (-2.0 / temper) for part in pair) for pair in columns]

    start = jnp.full((8, LANES), 1.0 / TASKS, jnp.float32)
    slope = [tree([steep[task][half] * (1.0 / TASKS) for task in range(TASKS)], jnp.add) for half in range(2)]
    mixture = [start, start]
    for iteration in range(ITERS):
        step = 2.0 / (iteration + 2.0)
        weight = [jnp.exp(half) for half in slope]
        rows = [row_of(weight, task) for task in range(TASKS)]
        scale = step / tree(rows, jnp.add)
        moved = [tree([steep[task][half] * rows[task] for task in range(TASKS)], jnp.add) for half in range(2)]
        slope = [(1.0 - step) * slope[half] + scale * moved[half] for half in range(2)]
        mixture = [(1.0 - step) * mixture[half] + scale * weight[half] for half in range(2)]
    return mixture


UPDATE_ROWS = 32


def spread_weights(mixes, group):
    size = TASKS * ROW_BLOCK
    row = lax.broadcasted_iota(jnp.int32, (ROW_BLOCK, size), 0)
    column = lax.broadcasted_iota(jnp.int32, (ROW_BLOCK, size), 1)
    lane = group * (LANES // 2)
    weights = jnp.zeros((ROW_BLOCK, size), jnp.float32)
    for task in range(TASKS):
        value = jnp.broadcast_to(mixes[task : task + 1, lane : lane + 1], (ROW_BLOCK, size))
        weights = jnp.where(column == task * ROW_BLOCK + row, value, weights)
    parts = []
    rest = weights
    for _ in range(3):
        part = rest.astype(jnp.bfloat16)
        parts.append(part)
        rest = rest - part.astype(jnp.float32)
    return jnp.concatenate(parts, axis=0)


def update_kernel(
    gram_ref,
    first_ref,
    second_ref,
    first_w,
    first_m,
    first_v,
    second_w,
    second_m,
    second_v,
    out_first_c,
    out_first_w,
    out_first_m,
    out_first_v,
    out_second_c,
    out_second_w,
    out_second_m,
    out_second_v,
    result,
    mixes,
    out_sem,
):
    stored = ((first_w, first_m, first_v), (second_w, second_m, second_v))
    outputs = (
        (out_first_c, out_first_w, out_first_m, out_first_v),
        (out_second_c, out_second_w, out_second_m, out_second_v),
    )
    mixture = frank_wolfe(gram_ref[...])
    for half in range(2):
        mixes[8 * half : 8 * half + 8, :] = mixture[half]

    rows_all, width = first_w.shape
    retained = (first_ref, second_ref)
    stores = []
    for group in range(2):
        weights_of = spread_weights(mixes, group)
        for block in range(rows_all // UPDATE_ROWS):
            rows = slice(block * UPDATE_ROWS, (block + 1) * UPDATE_ROWS)
            pieces = []
            for row in range(rows.start, rows.stop, ROW_BLOCK):
                side = retained[group][:, row : row + ROW_BLOCK, :].reshape(TASKS * ROW_BLOCK, width)
                product = jnp.dot(weights_of, side, preferred_element_type=jnp.float32)
                pieces.append(
                    product[:ROW_BLOCK] + (product[ROW_BLOCK : 2 * ROW_BLOCK] + product[2 * ROW_BLOCK :])
                )
            combined = jnp.concatenate(pieces, axis=0)
            weights = stored[group][0][rows, :]
            moment = stored[group][1][rows, :]
            variance = stored[group][2][rows, :]
            new_moment = beta_one * moment + (1.0 - beta_one) * combined
            new_variance = beta_two * variance + (1.0 - beta_two) * combined * combined
            moved = new_moment * (learn_rate / (1.0 - beta_one**adam_step))
            scaled_var = new_variance * (1.0 / (1.0 - beta_two**adam_step))
            new_weights = weights - moved / (jnp.sqrt(scaled_var) + epsilon)
            values = (combined, new_weights, new_moment, new_variance)
            for kind, value in enumerate(values):
                result[group, kind, rows, :] = value
                copy = pltpu.make_async_copy(
                    result.at[group, kind, rows, :],
                    outputs[group][kind].at[rows, :],
                    out_sem.at[group, block, kind],
                )
                copy.start()
                stores.append(copy)
    for copy in stores:
        copy.wait()


def local(
    grads_first,
    weights_first,
    moment_first,
    variance_first,
    grads_second,
    weights_second,
    moment_second,
    variance_second,
):
    held, rows, columns = grads_first.shape
    width = weights_first.shape[1]
    in_vmem = pl.BlockSpec(memory_space=pltpu.VMEM)
    in_hbm = pl.BlockSpec(memory_space=pltpu.HBM)
    tile = (8, LANES)
    packed = (4, LANES)
    first, second, gram = pl.pallas_call(
        exchange_kernel,
        name="exchange",
        out_shape=(
            pltpu.VMEM((TASKS, rows, width), jnp.bfloat16),
            pltpu.VMEM((TASKS, rows, width), jnp.bfloat16),
            pltpu.VMEM(tile, jnp.float32),
        ),
        in_specs=[in_hbm, in_hbm],
        out_specs=(in_vmem, in_vmem, in_vmem),
        scratch_shapes=[
            pltpu.VMEM((2,) + packed, jnp.float32),
            pltpu.VMEM((CHIPS_Y * CHIPS_X * CORES,) + packed, jnp.float32),
            pltpu.VMEM((CHIPS_Z,) + packed, jnp.float32),
            pltpu.SemaphoreType.DMA((len(PIECES),)),
            pltpu.SemaphoreType.DMA((len(PIECES),)),
            pltpu.SemaphoreType.DMA((2,)),
            pltpu.SemaphoreType.DMA((2,)),
            pltpu.SemaphoreType.REGULAR((4,)),
        ],
        compiler_params=pltpu.CompilerParams(
            collective_id=0, has_side_effects=True, vmem_limit_bytes=60 * 1000 * 1000
        ),
    )(grads_first, grads_second)

    shape = jax.ShapeDtypeStruct((rows, width), jnp.float32)
    return pl.pallas_call(
        update_kernel,
        name="update",
        out_shape=(shape,) * 8,
        in_specs=[in_vmem] * 9,
        out_specs=(in_hbm,) * 8,
        scratch_shapes=[
            pltpu.VMEM((2, 4, rows, width), jnp.float32),
            pltpu.VMEM((TASKS, LANES), jnp.float32),
            pltpu.SemaphoreType.DMA((2, rows // UPDATE_ROWS, 4)),
        ],
        compiler_params=pltpu.CompilerParams(vmem_limit_bytes=32 * 1024 * 1024),
    )(
        gram,
        first,
        second,
        weights_first,
        moment_first,
        variance_first,
        weights_second,
        moment_second,
        variance_second,
    )


def solution(mesh):
    in_specs = (
        P("task", "fsdp", None),
        P("fsdp", "task"),
        P("fsdp", "task"),
        P("fsdp", "task"),
        P("task", "fsdp", None),
        P("fsdp", "task"),
        P("fsdp", "task"),
        P("fsdp", "task"),
    )
    out_specs = (P("fsdp", "task"),) * 8
    return jax.shard_map(local, mesh=mesh, in_specs=in_specs, out_specs=out_specs, check_vma=False)
```
